32 devices in a mesh: space: 8 (over z, x), sub: 4 (over y, core).
Axes of the slice: x: 2, y: 2, z: 4, core: 2. Of those that a mesh axis runs over, the one named last changes fastest.
Arguments:
- multipole: float32 [8192, 152], P('space'), may hold values from -6 to 6
- inherited: float32 [8192, 152], P(('space', 'sub')), may hold values from -6 to 6
- send_rows: int32 [8, 4, 384], P('space'), may hold values from 0 to 1023
- sources: int32 [8192, 316], P('space', 'sub'), may hold values from -1 to 2559, as said below
- operators: float32 [316, 152, 152], P('sub'), may hold values from -0.0546875 to 0.0546875
Outputs:
- local: float32 [8192, 152], P(('space', 'sub'))
The draws below stay inside these ranges and needn't reach their ends.
Inputs may be any that keep to these rules, and one draw needn't show every extreme that they name: `sources`: an entry that names a ghost row names one whose sending block exists.
All inputs are finite; a program needn't handle non-finite values.
Results may differ from the reference program's by a relative error of at most 0.0003.
Values sent between devices are 32-bit elements; how exact they have to be, the bound alone decides.
A program may use at most 192 MiB of HBM per device.

```python
import jax
import jax.numpy as jnp
from jax import lax

COEF = 152
OPS_DEV = 79
OPS = 316
C_DEV = 1024
GH = 384
NEAR = 2
CELLS = 8192
BLOCKS = 8
N_SPACE = 8
N_SUB = 4


def draw_sources(key, part):
    keys = jax.random.split(key, 5)
    shape = (C_DEV * N_SPACE, OPS_DEV * N_SUB)
    present = jax.random.randint(keys[0], shape, 0, 10) < 6
    ghostly = jax.random.randint(keys[1], shape, 0, 2) == 1
    local_row = jax.random.randint(keys[2], shape, 0, C_DEV)
    peer_slot = jax.random.randint(keys[3], shape, 0, 2 * NEAR)
    slot_index = jax.random.randint(keys[4], shape, 0, GH)
    device = (jnp.arange(shape[0], dtype=jnp.int32) // C_DEV)[:, None]
    offset = jnp.where(peer_slot < NEAR, peer_slot + 1, NEAR - 1 - peer_slot)
    anchor = device - offset
    reachable = (anchor >= 0) & (anchor < N_SPACE)
    ghost_index = C_DEV + peer_slot * GH + slot_index
    value = jnp.where(ghostly, ghost_index, local_row)
    keep = present & (reachable | jnp.logical_not(ghostly))
    return jnp.where(keep, value, -1).astype(jnp.int32)


def plant(array, rng, smallest, top_value):
    longest = array.shape.index(max(array.shape))
    spots = []
    for shift in (0, 1):
        where = [jax.random.randint(jax.random.fold_in(rng, axis), (), 0, length) for axis, length in enumerate(array.shape)]
        where[longest] = (where[longest] + shift) % array.shape[longest]
        spots.append(tuple(where))
    return array.at[spots[0]].set(smallest).at[spots[1]].set(top_value)


def block_levels(rng, dims, cuts, least, high):
    def one(dim, parts):
        steps = jax.random.uniform(jax.random.fold_in(jax.random.fold_in(rng, 6), dim), (parts,), jnp.float32, least / len(cuts), high / len(cuts))
        return jnp.repeat(jnp.exp(steps), dims[dim] // parts).reshape((-1,) + (1,) * (len(dims) - dim - 1))

    gain = one(*cuts[0])
    for cut in cuts[1:]:
        gain = gain * one(*cut)
    return gain


def scatter_about(stream_key, shape, spread, most, shards=(), held_as=jnp.bfloat16):
    entries = jax.random.normal(stream_key, shape, jnp.float32) * spread
    if len(shards) > 0:
        entries = block_levels(stream_key, shape, shards, -0.22, 0.18) * entries
    return jnp.clip(entries, min=-most, max=most).astype(held_as)


def setup_inputs(seed: int = 0) -> dict:
    streams_of = jax.random.split(jax.random.key(seed), 6)
    multipole = scatter_about(streams_of[0], (CELLS, COEF), 1.0, 6.0, ((0, 8),), jnp.float32)
    inherited = scatter_about(streams_of[1], (CELLS, COEF), 1.0, 6.0, ((0, 32),), jnp.float32)
    send_rows = plant(jax.random.randint(streams_of[2], (BLOCKS, 2 * NEAR, GH), 0, C_DEV), jax.random.fold_in(streams_of[2], 1), 0, C_DEV - 1).astype(jnp.int32)
    sources = draw_sources(jax.random.fold_in(streams_of[5], 71), 0)
    operators = scatter_about(streams_of[4], (OPS, COEF, COEF), (COEF * OPS_DEV) ** -0.5, 0.0546875, ((0, 4),), jnp.float32)
    return dict(multipole=multipole, inherited=inherited, send_rows=send_rows, sources=sources, operators=operators)


def reference(multipole, inherited, send_rows, sources, operators):
    blocks = multipole.reshape(N_SPACE, C_DEV, COEF)
    flat_ops = operators.reshape(OPS_DEV * N_SUB * COEF, COEF)
    source_blocks = sources.reshape(N_SPACE, C_DEV, OPS_DEV * N_SUB)

    def one_device(pieces):
        device, index_block = pieces
        ghost_list = []
        for peer_slot in range(2 * NEAR):
            offset = peer_slot + 1 if peer_slot < NEAR else NEAR - 1 - peer_slot
            anchor = device - offset
            inside = (anchor >= 0) & (anchor < N_SPACE)
            safe_anchor = jnp.clip(anchor, 0, N_SPACE - 1).astype(jnp.int32)
            picked = blocks[safe_anchor][send_rows[safe_anchor, peer_slot]]
            ghost_list.append(jnp.where(inside, picked, jnp.zeros_like(picked)))
        lookup = jnp.concatenate([blocks[device]] + ghost_list, axis=0)
        present = index_block >= 0
        safe_index = jnp.where(present, index_block, 0).astype(jnp.int32)
        gathered = jnp.where(present[:, :, None], lookup[safe_index], jnp.zeros((), lookup.dtype))
        return jnp.dot(gathered.reshape(C_DEV, -1), flat_ops, precision=lax.Precision.HIGHEST, preferred_element_type=jnp.float32)

    partial_value = lax.map(one_device, (jnp.arange(N_SPACE, dtype=jnp.int32), source_blocks))
    return partial_value.reshape(C_DEV * N_SPACE, COEF) + inherited
```

```python
import functools

import jax
import jax.numpy as jnp
from jax import lax
from jax.experimental import pallas as pl
from jax.experimental.pallas import tpu as pltpu
from jax.sharding import PartitionSpec as P

LANES = 128


def passed_along(block, axis, distance):
    devices = range(lax.axis_size(axis))
    route = [(i - distance, i) for i in devices if i - distance in devices]
    return lax.ppermute(block, axis, route)


def translate(width, rows, ids, prev_op, this_op, table, out, odd, even):
    tail = width - LANES
    step = pl.program_id(0)

    @pl.when(step == 0)
    def _():
        out[...] = jnp.zeros_like(out)
        odd[...] = jnp.zeros_like(odd)

    def gather(half, target):
        for r in range(rows):
            target[r] = table[ids[0, 0, half * rows + r]]

    def weights(op):
        full = op[0]
        high = full.astype(jnp.bfloat16).astype(jnp.float32)
        low = full - high
        pad = jnp.zeros((LANES // 4 - tail, width), jnp.float32)
        end = jnp.zeros((LANES // 4, width), jnp.float32)
        mix = jnp.concatenate(
            [high[LANES:], pad, high[LANES:], pad, low[LANES:], pad, end], axis=0
        )
        first = high[:LANES].astype(jnp.bfloat16)
        second = low[:LANES].astype(jnp.bfloat16)
        return (
            jnp.concatenate([first, first], axis=0),
            jnp.concatenate([second, mix.astype(jnp.bfloat16)], axis=0),
        )

    def product(op, source):
        flat = source.reshape(2 * rows, LANES)
        head = flat[pl.ds(0, rows, stride=2), :]
        rest = flat[pl.ds(1, rows, stride=2), :]
        head_high = head.astype(jnp.bfloat16)
        head_low = (head - head_high.astype(jnp.float32)).astype(jnp.bfloat16)
        rest_high = rest.astype(jnp.bfloat16).astype(jnp.float32)
        lane = lax.broadcasted_iota(jnp.int32, rest.shape, 1)
        second = (lane >= LANES // 4) & (lane < LANES // 2)
        rest_mix = jnp.where(second, rest - rest_high, rest_high).astype(jnp.bfloat16)
        first_w, second_w = weights(op)
        out[...] += jnp.dot(
            jnp.concatenate([head_high, head_low], axis=1),
            first_w,
            preferred_element_type=jnp.float32,
        ) + jnp.dot(
            jnp.concatenate([head_high, rest_mix], axis=1),
            second_w,
            preferred_element_type=jnp.float32,
        )

    gather(0, even)
    product(prev_op, odd)
    gather(1, odd)
    product(this_op, even)


def partial_sum(table, ids, operators, rows):
    count, width, _ = operators.shape
    steps = ids.shape[0]
    return pl.pallas_call(
        functools.partial(translate, width, rows),
        grid=(steps,),
        in_specs=[
            pl.BlockSpec((1, 1, 2 * rows), lambda i: (i, 0, 0), memory_space=pltpu.SMEM),
            pl.BlockSpec((1, width, width), lambda i: (jnp.maximum(2 * i - 1, 0), 0, 0)),
            pl.BlockSpec((1, width, width), lambda i: (jnp.minimum(2 * i, count - 1), 0, 0)),
            pl.BlockSpec(memory_space=pltpu.VMEM),
        ],
        out_specs=pl.BlockSpec((rows, width), lambda i: (0, 0)),
        out_shape=jax.ShapeDtypeStruct((rows, width), jnp.float32),
        scratch_shapes=[
            pltpu.VMEM((rows, 2, LANES), jnp.float32),
            pltpu.VMEM((rows, 2, LANES), jnp.float32),
        ],
        compiler_params=pltpu.CompilerParams(
            dimension_semantics=("arbitrary",), vmem_limit_bytes=48 * 1024 * 1024
        ),
    )(ids, operators, operators, table)


def local(multipole, inherited, send_rows, sources, operators):
    near_count = send_rows.shape[1] // 2
    rows, width = multipole.shape
    count = operators.shape[0]
    tail = width - LANES
    gap = jnp.zeros((rows, LANES // 4 - tail), jnp.float32)
    end = multipole[:, LANES:]
    wide = jnp.concatenate(
        [multipole[:, :LANES], end, gap, end, gap, end, gap, jnp.zeros((rows, LANES // 4), jnp.float32)], axis=1
    )
    send_map = send_rows[0]
    payloads = [wide]
    for peer_slot in range(2 * near_count):
        offset = peer_slot + 1 if peer_slot < near_count else near_count - 1 - peer_slot
        payloads.append(passed_along(wide[send_map[peer_slot]], "space", offset))
    payloads.append(jnp.zeros((8, 2 * LANES), jnp.float32))
    table = jnp.concatenate(payloads, axis=0)
    empty_row = table.shape[0] - 8
    table = table.reshape(-1, 2, LANES)

    steps = count // 2 + 1
    safe = jnp.where(sources >= 0, sources, empty_row)
    safe = jnp.pad(safe, ((0, 0), (0, 2 * steps - count)), constant_values=empty_row)
    ids = safe.T.reshape(steps, 1, 2 * rows)
    total = partial_sum(table, ids, operators, rows)
    summed = lax.psum_scatter(total, "sub", scatter_dimension=0, tiled=True)
    return summed + inherited


def solution(mesh):
    return jax.shard_map(
        local,
        mesh=mesh,
        in_specs=(
            P("space", None),
            P(("space", "sub"), None),
            P("space", None, None),
            P("space", "sub"),
            P("sub", None, None),
        ),
        out_specs=P(("space", "sub"), None),
        check_vma=False,
    )
```

```python
import functools

import jax
import jax.numpy as jnp
from jax import lax
from jax.experimental import pallas as pl
from jax.experimental.pallas import tpu as pltpu
from jax.sharding import PartitionSpec as P

LANES = 128


def passed_along(block, axis, distance):
    devices = range(lax.axis_size(axis))
    route = [(i - distance, i) for i in devices if i - distance in devices]
    return lax.ppermute(block, axis, route)


def translate(width, rows, ids, op, block, *refs):
    ghosts, (out, table, odd, even) = refs[:-4], refs[-4:]
    tail = width - LANES
    step = pl.program_id(0)
    flat_table = table.reshape(2 * table.shape[0], LANES)

    def widen(part, start):
        count = part.shape[0]
        flat_table[pl.ds(2 * start, count, stride=2), :] = part[:, :LANES]
        rest = jnp.concatenate(
            [part[:, LANES:], jnp.zeros((count, LANES - tail), jnp.float32)], axis=1
        )
        spread = rest + pltpu.roll(rest, LANES // 4, 1) + pltpu.roll(rest, LANES // 2, 1)
        flat_table[pl.ds(2 * start + 1, count, stride=2), :] = spread

    @pl.when(step == 0)
    def _():
        out[...] = jnp.zeros_like(out)
        odd[...] = jnp.zeros_like(odd)
        start = 0
        for part in (block, *ghosts):
            widen(part, start)
            start += part.shape[0]
        flat_table[2 * start :, :] = jnp.zeros((2 * (table.shape[0] - start), LANES), jnp.float32)

    def gather(half, target):
        for r in range(rows):
            target[r] = table[ids[0, 0, half * rows + r]]

    def weights(index):
        full = op[index]
        high = full.astype(jnp.bfloat16).astype(jnp.float32)
        low = full - high
        pad = jnp.zeros((LANES // 4 - tail, width), jnp.float32)
        end = jnp.zeros((LANES // 4, width), jnp.float32)
        mix = jnp.concatenate(
            [high[LANES:], pad, high[LANES:], pad, low[LANES:], pad, end], axis=0
        )
        first = high[:LANES].astype(jnp.bfloat16)
        second = low[:LANES].astype(jnp.bfloat16)
        return jnp.concatenate([first, first, second, mix.astype(jnp.bfloat16)], axis=0)

    def product(index, source):
        flat = source.reshape(2 * rows, LANES)
        head = flat[pl.ds(0, rows, stride=2), :]
        rest = flat[pl.ds(1, rows, stride=2), :]
        head_high = head.astype(jnp.bfloat16)
        head_low = (head - head_high.astype(jnp.float32)).astype(jnp.bfloat16)
        rest_high = rest.astype(jnp.bfloat16).astype(jnp.float32)
        lane = lax.broadcasted_iota(jnp.int32, rest.shape, 1)
        second = (lane >= LANES // 4) & (lane < LANES // 2)
        rest_mix = jnp.where(second, rest - rest_high, rest_high).astype(jnp.bfloat16)
        out[...] += jnp.dot(
            jnp.concatenate([head_high, head_low, head_high, rest_mix], axis=1),
            weights(index),
            preferred_element_type=jnp.float32,
        )

    gather(0, even)
    product(jnp.maximum(2 * step - 1, 0), odd)
    gather(1, odd)
    product(jnp.minimum(2 * step, op.shape[0] - 1), even)


def partial_sum(block, ghosts, ids, operators):
    rows, width = block.shape
    steps = ids.shape[0]
    table_rows = rows + sum(g.shape[0] for g in ghosts) + 8
    whole = pl.BlockSpec(memory_space=pltpu.VMEM)
    return pl.pallas_call(
        functools.partial(translate, width, rows),
        grid=(steps,),
        in_specs=[
            pl.BlockSpec((1, 1, 2 * rows), lambda i: (i, 0, 0), memory_space=pltpu.SMEM),
        ]
        + [whole] * (2 + len(ghosts)),
        out_specs=pl.BlockSpec((rows, width), lambda i: (0, 0)),
        out_shape=jax.ShapeDtypeStruct((rows, width), jnp.float32),
        scratch_shapes=[
            pltpu.VMEM((table_rows, 2, LANES), jnp.float32),
            pltpu.VMEM((rows, 2, LANES), jnp.float32),
            pltpu.VMEM((rows, 2, LANES), jnp.float32),
        ],
        compiler_params=pltpu.CompilerParams(
            dimension_semantics=("arbitrary",), vmem_limit_bytes=48 * 1024 * 1024
        ),
    )(ids, operators, block, *ghosts)


def reduce_scatter(n, total, inherited, out, outgoing, incoming, send_sems, recv_sems):
    space, me = lax.axis_index("space"), lax.axis_index("sub")
    chunk = out.shape[1]
    peers = [lax.rem(me + k, n) for k in range(1, n)]
    barrier = pltpu.get_barrier_semaphore()
    for peer in peers:
        pl.semaphore_signal(
            barrier, inc=1, device_id=(space, peer), device_id_type=pl.DeviceIdType.MESH
        )
    pl.semaphore_wait(barrier, n - 1)
    copies = []
    for k, peer in enumerate(peers):
        outgoing[k] = total[pl.ds(pl.multiple_of(peer * chunk, chunk), chunk), :].T
        copy = pltpu.make_async_remote_copy(
            src_ref=outgoing.at[k],
            dst_ref=incoming.at[k],
            send_sem=send_sems.at[k],
            recv_sem=recv_sems.at[k],
            device_id=(space, peer),
            device_id_type=pl.DeviceIdType.MESH,
        )
        copy.start()
        copies.append(copy)
    out[...] = inherited[...] + total[pl.ds(pl.multiple_of(me * chunk, chunk), chunk), :].T
    for k, copy in enumerate(copies):
        copy.wait()
        out[...] += incoming[k]


def scatter_sum(total, inherited, n):
    width, chunk = inherited.shape
    whole = pl.BlockSpec(memory_space=pltpu.VMEM)
    return pl.pallas_call(
        functools.partial(reduce_scatter, n),
        in_specs=[whole] * 2,
        out_specs=whole,
        out_shape=jax.ShapeDtypeStruct((width, chunk), jnp.float32),
        scratch_shapes=[
            pltpu.VMEM((n - 1, width, chunk), jnp.float32),
            pltpu.VMEM((n - 1, width, chunk), jnp.float32),
            pltpu.SemaphoreType.DMA((n - 1,)),
            pltpu.SemaphoreType.DMA((n - 1,)),
        ],
        compiler_params=pltpu.CompilerParams(collective_id=0, has_side_effects=True),
    )(total, inherited)


def local(multipole, inherited, send_rows, sources, operators):
    near_count = send_rows.shape[1] // 2
    rows = multipole.shape[0]
    count = operators.shape[0]
    send_map = send_rows[0]
    picked = multipole[send_map.reshape(-1)].reshape(*send_map.shape, -1)
    ghosts = []
    for peer_slot in range(2 * near_count):
        offset = peer_slot + 1 if peer_slot < near_count else near_count - 1 - peer_slot
        ghosts.append(passed_along(picked[peer_slot], "space", offset))
    empty_row = rows + send_map.size
    steps = count // 2 + 1
    safe = jnp.where(sources >= 0, sources, empty_row)
    safe = jnp.pad(safe, ((0, 0), (0, 2 * steps - count)), constant_values=empty_row)
    ids = safe.T.reshape(steps, 1, 2 * rows)
    total = partial_sum(multipole, ghosts, ids, operators)
    return scatter_sum(total, inherited.T, lax.axis_size("sub")).T


def solution(mesh):
    return jax.shard_map(
        local,
        mesh=mesh,
        in_specs=(
            P("space", None),
            P(("space", "sub"), None),
            P("space", None, None),
            P("space", "sub"),
            P("sub", None, None),
        ),
        out_specs=P(("space", "sub"), None),
        check_vma=False,
    )
```

```python
import functools

import jax
import jax.numpy as jnp
from jax import lax
from jax.experimental import pallas as pl
from jax.experimental.pallas import tpu as pltpu
from jax.sharding import PartitionSpec as P

LANES = 128


def passed_along(block, axis, distance):
    devices = range(lax.axis_size(axis))
    route = [(i - distance, i) for i in devices if i - distance in devices]
    return lax.ppermute(block, axis, route)


def translate(width, rows, ids, op, block, *refs):
    ghosts, (out, table, odd, even) = refs[:-4], refs[-4:]
    tail = width - LANES
    step = pl.program_id(0)
    flat_table = table.reshape(2 * table.shape[0], LANES)

    def widen(part, start):
        count = part.shape[0]
        flat_table[pl.ds(2 * start, count, stride=2), :] = part[:, :LANES]
        rest = jnp.concatenate(
            [part[:, LANES:], jnp.zeros((count, LANES - tail), jnp.float32)], axis=1
        )
        spread = rest + pltpu.roll(rest, LANES // 4, 1) + pltpu.roll(rest, LANES // 2, 1)
        flat_table[pl.ds(2 * start + 1, count, stride=2), :] = spread

    @pl.when(step == 0)
    def _():
        out[...] = jnp.zeros_like(out)
        odd[...] = jnp.zeros_like(odd)
        start = 0
        for part in (block, *ghosts):
            widen(part, start)
            start += part.shape[0]
        flat_table[2 * start :, :] = jnp.zeros((2 * (table.shape[0] - start), LANES), jnp.float32)

    def gather(half, target):
        for r in range(rows):
            target[r] = flat_table[pl.ds(pl.multiple_of(ids[0, 0, half * rows + r], 2), 2), :]

    def weights(index):
        full = op[index]
        high = full.astype(jnp.bfloat16).astype(jnp.float32)
        low = full - high
        pad = jnp.zeros((LANES // 4 - tail, width), jnp.float32)
        end = jnp.zeros((LANES // 4, width), jnp.float32)
        mix = jnp.concatenate(
            [high[LANES:], pad, high[LANES:], pad, low[LANES:], pad, end], axis=0
        )
        first = high[:LANES].astype(jnp.bfloat16)
        second = low[:LANES].astype(jnp.bfloat16)
        return jnp.concatenate([first, first, second, mix.astype(jnp.bfloat16)], axis=0)

    def product(index, source):
        flat = source.reshape(2 * rows, LANES)
        head = flat[pl.ds(0, rows, stride=2), :]
        rest = flat[pl.ds(1, rows, stride=2), :]
        head_high = head.astype(jnp.bfloat16)
        head_low = (head - head_high.astype(jnp.float32)).astype(jnp.bfloat16)
        rest_high = rest.astype(jnp.bfloat16).astype(jnp.float32)
        lane = lax.broadcasted_iota(jnp.int32, rest.shape, 1)
        second = (lane >= LANES // 4) & (lane < LANES // 2)
        rest_mix = jnp.where(second, rest - rest_high, rest_high).astype(jnp.bfloat16)
        out[...] += jnp.dot(
            jnp.concatenate([head_high, head_low, head_high, rest_mix], axis=1),
            weights(index),
            preferred_element_type=jnp.float32,
        )

    gather(0, even)
    product(jnp.maximum(2 * step - 1, 0), odd)
    gather(1, odd)
    product(jnp.minimum(2 * step, op.shape[0] - 1), even)


def partial_sum(block, ghosts, ids, operators):
    rows, width = block.shape
    steps = ids.shape[0]
    table_rows = rows + sum(g.shape[0] for g in ghosts) + 8
    whole = pl.BlockSpec(memory_space=pltpu.VMEM)
    return pl.pallas_call(
        functools.partial(translate, width, rows),
        grid=(steps,),
        in_specs=[
            pl.BlockSpec((1, 1, 2 * rows), lambda i: (i, 0, 0), memory_space=pltpu.SMEM),
        ]
        + [whole] * (2 + len(ghosts)),
        out_specs=pl.BlockSpec((rows, width), lambda i: (0, 0)),
        out_shape=jax.ShapeDtypeStruct((rows, width), jnp.float32),
        scratch_shapes=[
            pltpu.VMEM((table_rows, 2, LANES), jnp.float32),
            pltpu.VMEM((rows, 2, LANES), jnp.float32),
            pltpu.VMEM((rows, 2, LANES), jnp.float32),
        ],
        compiler_params=pltpu.CompilerParams(
            dimension_semantics=("arbitrary",), vmem_limit_bytes=48 * 1024 * 1024
        ),
    )(ids, operators, block, *ghosts)


def reduce_scatter(n, total, inherited, out, outgoing, incoming, send_sems, recv_sems):
    space, me = lax.axis_index("space"), lax.axis_index("sub")
    chunk = out.shape[1]
    peers = [lax.rem(me + k, n) for k in range(1, n)]
    barrier = pltpu.get_barrier_semaphore()
    for peer in peers:
        pl.semaphore_signal(
            barrier, inc=1, device_id=(space, peer), device_id_type=pl.DeviceIdType.MESH
        )
    pl.semaphore_wait(barrier, n - 1)
    copies = []
    for k, peer in enumerate(peers):
        outgoing[k] = total[pl.ds(pl.multiple_of(peer * chunk, chunk), chunk), :].T
        copy = pltpu.make_async_remote_copy(
            src_ref=outgoing.at[k],
            dst_ref=incoming.at[k],
            send_sem=send_sems.at[k],
            recv_sem=recv_sems.at[k],
            device_id=(space, peer),
            device_id_type=pl.DeviceIdType.MESH,
        )
        copy.start()
        copies.append(copy)
    out[...] = inherited[...] + total[pl.ds(pl.multiple_of(me * chunk, chunk), chunk), :].T
    for k, copy in enumerate(copies):
        copy.wait()
        out[...] += incoming[k]


def scatter_sum(total, inherited, n):
    width, chunk = inherited.shape
    whole = pl.BlockSpec(memory_space=pltpu.VMEM)
    return pl.pallas_call(
        functools.partial(reduce_scatter, n),
        in_specs=[whole] * 2,
        out_specs=whole,
        out_shape=jax.ShapeDtypeStruct((width, chunk), jnp.float32),
        scratch_shapes=[
            pltpu.VMEM((n - 1, width, chunk), jnp.float32),
            pltpu.VMEM((n - 1, width, chunk), jnp.float32),
            pltpu.SemaphoreType.DMA((n - 1,)),
            pltpu.SemaphoreType.DMA((n - 1,)),
        ],
        compiler_params=pltpu.CompilerParams(collective_id=0, has_side_effects=True),
    )(total, inherited)


def local(multipole, inherited, send_rows, sources, operators):
    near_count = send_rows.shape[1] // 2
    rows = multipole.shape[0]
    count = operators.shape[0]
    send_map = send_rows[0]
    picked = multipole[send_map.reshape(-1)].reshape(*send_map.shape, -1)
    ghosts = []
    for peer_slot in range(2 * near_count):
        offset = peer_slot + 1 if peer_slot < near_count else near_count - 1 - peer_slot
        ghosts.append(passed_along(picked[peer_slot], "space", offset))
    empty_row = rows + send_map.size
    steps = count // 2 + 1
    safe = jnp.where(sources >= 0, sources, empty_row)
    safe = jnp.pad(safe, ((0, 0), (0, 2 * steps - count)), constant_values=empty_row)
    ids = (2 * safe).T.reshape(steps, 1, 2 * rows)
    total = partial_sum(multipole, ghosts, ids, operators)
    return scatter_sum(total, inherited.T, lax.axis_size("sub")).T


def solution(mesh):
    return jax.shard_map(
        local,
        mesh=mesh,
        in_specs=(
            P("space", None),
            P(("space", "sub"), None),
            P("space", None, None),
            P("space", "sub"),
            P("sub", None, None),
        ),
        out_specs=P(("space", "sub"), None),
        check_vma=False,
    )
```

```python
import functools

import jax
import jax.numpy as jnp
from jax import lax
from jax.experimental import pallas as pl
from jax.experimental.pallas import tpu as pltpu
from jax.sharding import PartitionSpec as P

LANES = 128


def passed_along(block, axis, distance):
    devices = range(lax.axis_size(axis))
    route = [(i - distance, i) for i in devices if i - distance in devices]
    return lax.ppermute(block, axis, route)


def translate(width, rows, ids, op, block, *refs):
    ghosts, (out, table, odd, even, op_head, op_rest) = refs[:-6], refs[-6:]
    count = op.shape[2]
    stride = op_head.shape[0] // (width + 1)
    tail = width - LANES
    step = pl.program_id(0)
    flat_table = table.reshape(2 * table.shape[0], LANES)

    def widen(part, start):
        count = part.shape[0]
        flat_table[pl.ds(2 * start, count, stride=2), :] = part[:, :LANES]
        rest = jnp.concatenate(
            [part[:, LANES:], jnp.zeros((count, LANES - tail), jnp.float32)], axis=1
        )
        spread = rest + pltpu.roll(rest, LANES // 4, 1) + pltpu.roll(rest, LANES // 2, 1)
        flat_table[pl.ds(2 * start + 1, count, stride=2), :] = spread

    @pl.when(step == 0)
    def _():
        out[...] = jnp.zeros_like(out)
        odd[...] = jnp.zeros_like(odd)
        start = 0
        for part in (block, *ghosts):
            widen(part, start)
            start += part.shape[0]
        def turn(i, carry):
            turned = op[i].T
            place = pl.ds(pl.multiple_of(i * stride, 8), count)
            op_head[place, :] = turned[:, :LANES]
            op_rest[place, :tail] = turned[:, LANES:]
            return carry

        lax.fori_loop(0, width, turn, 0, unroll=8)
        flat_table[2 * start :, :] = jnp.zeros((2 * (table.shape[0] - start), LANES), jnp.float32)

    def gather(half, target):
        for r in range(rows):
            target[r] = flat_table[pl.ds(pl.multiple_of(ids[0, 0, half * rows + r], 2), 2), :]

    def weights(index):
        every = pl.ds(index, width, stride=stride)
        full = jnp.concatenate([op_head[every, :], op_rest[every, :][:, :tail]], axis=1)
        high = full.astype(jnp.bfloat16).astype(jnp.float32)
        low = full - high
        pad = jnp.zeros((LANES // 4 - tail, width), jnp.float32)
        end = jnp.zeros((LANES // 4, width), jnp.float32)
        mix = jnp.concatenate(
            [high[LANES:], pad, high[LANES:], pad, low[LANES:], pad, end], axis=0
        )
        first = high[:LANES].astype(jnp.bfloat16)
        second = low[:LANES].astype(jnp.bfloat16)
        return jnp.concatenate([first, first, second, mix.astype(jnp.bfloat16)], axis=0)

    def product(index, source):
        flat = source.reshape(2 * rows, LANES)
        head = flat[pl.ds(0, rows, stride=2), :]
        rest = flat[pl.ds(1, rows, stride=2), :]
        head_high = head.astype(jnp.bfloat16)
        head_low = (head - head_high.astype(jnp.float32)).astype(jnp.bfloat16)
        rest_high = rest.astype(jnp.bfloat16).astype(jnp.float32)
        lane = lax.broadcasted_iota(jnp.int32, rest.shape, 1)
        second = (lane >= LANES // 4) & (lane < LANES // 2)
        rest_mix = jnp.where(second, rest - rest_high, rest_high).astype(jnp.bfloat16)
        out[...] += jnp.dot(
            jnp.concatenate([head_high, head_low, head_high, rest_mix], axis=1),
            weights(index),
            preferred_element_type=jnp.float32,
        )

    gather(0, even)
    product(jnp.maximum(2 * step - 1, 0), odd)
    gather(1, odd)
    product(jnp.minimum(2 * step, count - 1), even)


def partial_sum(block, ghosts, ids, operators):
    rows, width = block.shape
    steps = ids.shape[0]
    op_stride = -(-operators.shape[0] // 8) * 8
    table_rows = rows + sum(g.shape[0] for g in ghosts) + 8
    whole = pl.BlockSpec(memory_space=pltpu.VMEM)
    return pl.pallas_call(
        functools.partial(translate, width, rows),
        grid=(steps,),
        in_specs=[
            pl.BlockSpec((1, 1, 2 * rows), lambda i: (i, 0, 0), memory_space=pltpu.SMEM),
        ]
        + [whole] * (2 + len(ghosts)),
        out_specs=pl.BlockSpec((rows, width), lambda i: (0, 0)),
        out_shape=jax.ShapeDtypeStruct((rows, width), jnp.float32),
        scratch_shapes=[
            pltpu.VMEM((table_rows, 2, LANES), jnp.float32),
            pltpu.VMEM((rows, 2, LANES), jnp.float32),
            pltpu.VMEM((rows, 2, LANES), jnp.float32),
            pltpu.VMEM(((width + 1) * op_stride, LANES), jnp.float32),
            pltpu.VMEM(((width + 1) * op_stride, LANES), jnp.float32),
        ],
        compiler_params=pltpu.CompilerParams(
            dimension_semantics=("arbitrary",), vmem_limit_bytes=48 * 1024 * 1024
        ),
    )(ids, operators.transpose(1, 2, 0), block, *ghosts)


def reduce_scatter(n, total, inherited, out, outgoing, incoming, send_sems, recv_sems):
    space, me = lax.axis_index("space"), lax.axis_index("sub")
    chunk = out.shape[1]
    peers = [lax.rem(me + k, n) for k in range(1, n)]
    barrier = pltpu.get_barrier_semaphore()
    for peer in peers:
        pl.semaphore_signal(
            barrier, inc=1, device_id=(space, peer), device_id_type=pl.DeviceIdType.MESH
        )
    pl.semaphore_wait(barrier, n - 1)
    copies = []
    for k, peer in enumerate(peers):
        outgoing[k] = total[pl.ds(pl.multiple_of(peer * chunk, chunk), chunk), :].T
        copy = pltpu.make_async_remote_copy(
            src_ref=outgoing.at[k],
            dst_ref=incoming.at[k],
            send_sem=send_sems.at[k],
            recv_sem=recv_sems.at[k],
            device_id=(space, peer),
            device_id_type=pl.DeviceIdType.MESH,
        )
        copy.start()
        copies.append(copy)
    out[...] = inherited[...] + total[pl.ds(pl.multiple_of(me * chunk, chunk), chunk), :].T
    for k, copy in enumerate(copies):
        copy.wait()
        out[...] += incoming[k]


def scatter_sum(total, inherited, n):
    width, chunk = inherited.shape
    whole = pl.BlockSpec(memory_space=pltpu.VMEM)
    return pl.pallas_call(
        functools.partial(reduce_scatter, n),
        in_specs=[whole] * 2,
        out_specs=whole,
        out_shape=jax.ShapeDtypeStruct((width, chunk), jnp.float32),
        scratch_shapes=[
            pltpu.VMEM((n - 1, width, chunk), jnp.float32),
            pltpu.VMEM((n - 1, width, chunk), jnp.float32),
            pltpu.SemaphoreType.DMA((n - 1,)),
            pltpu.SemaphoreType.DMA((n - 1,)),
        ],
        compiler_params=pltpu.CompilerParams(collective_id=0, has_side_effects=True),
    )(total, inherited)


def local(multipole, inherited, send_rows, sources, operators):
    near_count = send_rows.shape[1] // 2
    rows = multipole.shape[0]
    count = operators.shape[0]
    send_map = send_rows[0]
    picked = multipole[send_map.reshape(-1)].reshape(*send_map.shape, -1)
    ghosts = []
    for peer_slot in range(2 * near_count):
        offset = peer_slot + 1 if peer_slot < near_count else near_count - 1 - peer_slot
        ghosts.append(passed_along(picked[peer_slot], "space", offset))
    empty_row = rows + send_map.size
    steps = count // 2 + 1
    safe = jnp.where(sources >= 0, sources, empty_row)
    safe = jnp.pad(safe, ((0, 0), (0, 2 * steps - count)), constant_values=empty_row)
    ids = (2 * safe).T.reshape(steps, 1, 2 * rows)
    total = partial_sum(multipole, ghosts, ids, operators)
    return scatter_sum(total, inherited.T, lax.axis_size("sub")).T


def solution(mesh):
    return jax.shard_map(
        local,
        mesh=mesh,
        in_specs=(
            P("space", None),
            P(("space", "sub"), None),
            P("space", None, None),
            P("space", "sub"),
            P("sub", None, None),
        ),
        out_specs=P(("space", "sub"), None),
        check_vma=False,
    )
```
